256 devices in a mesh: layer: 8 (over z_lo, y), cell: 32 (over z_hi, x, core).
Axes of the slice: x: 4, y: 4, z: 8 (z_hi: 4, z_lo: 2; z = z_hi * 2 + z_lo), core: 2. Of those that a mesh axis runs over, the one named last changes fastest.
Arguments:
- shower_state: float32 [2, 48, 1024], P(None, 'layer', 'cell'), may hold values from -6 to 6
- cell_valid: int32 [1024], replicated, may hold values 0 or 1
- layer_valid: int32 [48], replicated, may hold values 0 or 1
- energy_bin: int32 [2], replicated, may hold values from 0 to 63
- time_index: int32 [1], replicated, may hold values from 0 to 999
- embed_weight: float32 [512], replicated, may hold values from -6 to 6
- cell_embed: float32 [1024, 512], P('cell'), may hold values from -6 to 6
- layer_embed: float32 [48, 512], P('layer'), may hold values from -6 to 6
- energy_table: float32 [64, 512], replicated, may hold values from -6 to 6
- gain_cells: float32 [512], replicated, may hold values from 0.1 to 1.9
- cell_heads: bfloat16 [512, 1536], replicated, may hold values from -0.25 to 0.25
- cell_merge: bfloat16 [512, 512], replicated, may hold values from -0.25 to 0.25
- cell_scale: float32 [8], replicated, may hold values from 0.5 to 40
- gain_layers: float32 [512], replicated, may hold values from 0.1 to 1.9
- layer_heads: bfloat16 [512, 1536], replicated, may hold values from -0.25 to 0.25
- layer_merge: bfloat16 [512, 512], replicated, may hold values from -0.25 to 0.25
- layer_scale: float32 [8], replicated, may hold values from 0.5 to 40
- gain_expand: float32 [512], replicated, may hold values from 0.1 to 1.9
- expand_weight: bfloat16 [512, 2048], replicated, may hold values from -0.25 to 0.25
- reduce_weight: bfloat16 [2048, 512], replicated, may hold values from -0.125 to 0.125
- gain_final: float32 [512], replicated, may hold values from 0.1 to 1.9
- velocity_head: float32 [512], replicated, may hold values from -0.25 to 0.25
Outputs:
- velocity: float32 [2, 48, 1024], P(None, 'layer', 'cell')
- next_state: float32 [2, 48, 1024], P(None, 'layer', 'cell')
The draws below stay inside these ranges and needn't reach their ends.
All inputs are finite; a program needn't handle non-finite values.
Results may differ from the reference program's by a relative error of at most 0.018.
The reference program's roundings to bfloat16 on the way count: a program that leaves them out, or rounds other values in their place, can miss the bound.
Values may be sent and summed in bfloat16 or wider, within the bound.
A program may use at most 192 MiB of HBM per device.

```python
import math
import jax
import jax.numpy as jnp
from jax import lax

D = 512
HEADS = 8
HDIM = 64
FF = 2048
NBINS = 64
GRID = 1000
STEPS = 2
SHOWERS = 2
LAYERS = 48
CELLS = 1024


def draw_scales(key):
    return jnp.exp(jax.random.uniform(key, (HEADS,), jnp.float32, math.log(0.5), math.log(4.0)))


def draw_cell_scale(key, part):
    return draw_scales(jax.random.fold_in(key, 11))


def draw_layer_scale(key, part):
    return draw_scales(jax.random.fold_in(key, 23))


def place_ends(values, stream_key, smallest, top_value):
    shape = values.shape
    place = [jax.random.randint(jax.random.fold_in(stream_key, axis), (), 0, shape[axis]) for axis in range(len(shape))]
    values = values.at[tuple(place)].set(smallest)
    longest = shape.index(max(shape))
    place[longest] = (place[longest] + 1) % shape[longest]
    return values.at[tuple(place)].set(top_value)


def levels(key, extent, cuts, least, largest):
    level, own = 1.0, jax.random.fold_in(key, 6)
    for axis_at, blocks in cuts:
        steps = jnp.exp(jax.random.uniform(jax.random.fold_in(own, axis_at), (blocks,), jnp.float32, least / len(cuts), largest / len(cuts)))
        level = level * jnp.repeat(steps, extent[axis_at] // blocks).reshape([-1 if axis == axis_at else 1 for axis in range(len(extent))])
    return level


def bell_draw(key, extent, spread, reach, cuts=(), held_as=jnp.bfloat16):
    result = jax.random.normal(key, extent, jnp.float32) * spread
    if len(cuts) > 0:
        result = levels(key, extent, cuts, -0.22, 0.18) * result
    return jnp.clip(result, min=-reach, max=reach).astype(held_as)


def setup_inputs(seed: int = 0) -> dict:
    key_list = jax.random.split(jax.random.key(seed), 23)
    return {
        "shower_state": bell_draw(key_list[0], (SHOWERS, LAYERS, CELLS), 1.0, 6.0, ((1, 8), (2, 32)), jnp.float32),
        "cell_valid": place_ends((jax.random.randint(key_list[1], (CELLS,), 0, 8) < 7).astype(jnp.int32), jax.random.fold_in(key_list[1], 1), 0, 1),
        "layer_valid": place_ends((jax.random.randint(key_list[2], (LAYERS,), 0, 16) < 15).astype(jnp.int32), jax.random.fold_in(key_list[2], 1), 0, 1),
        "energy_bin": jax.random.randint(key_list[3], (SHOWERS,), 0, NBINS).astype(jnp.int32),
        "time_index": jax.random.randint(key_list[4], (1,), 0, GRID).astype(jnp.int32),
        "embed_weight": bell_draw(key_list[5], (D,), 1.0, 6.0, (), jnp.float32),
        "cell_embed": bell_draw(key_list[6], (CELLS, D), 1.0, 6.0, ((0, 32),), jnp.float32),
        "layer_embed": bell_draw(key_list[7], (LAYERS, D), 1.0, 6.0, ((0, 8),), jnp.float32),
        "energy_table": bell_draw(key_list[8], (NBINS, D), 1.0, 6.0, (), jnp.float32),
        "gain_cells": jnp.clip(1.0 + 0.18 * jax.random.normal(key_list[9], (D,), jnp.float32), 0.1, 1.9),
        "cell_heads": bell_draw(key_list[10], (D, 3 * D), D ** -0.5, 0.25),
        "cell_merge": bell_draw(key_list[11], (D, D), D ** -0.5, 0.25),
        "cell_scale": draw_cell_scale(jax.random.fold_in(key_list[22], 71), 0),
        "gain_layers": jnp.clip(1.0 + 0.18 * jax.random.normal(key_list[13], (D,), jnp.float32), 0.1, 1.9),
        "layer_heads": bell_draw(key_list[14], (D, 3 * D), D ** -0.5, 0.25),
        "layer_merge": bell_draw(key_list[15], (D, D), D ** -0.5, 0.25),
        "layer_scale": draw_layer_scale(jax.random.fold_in(key_list[22], 71), 0),
        "gain_expand": jnp.clip(1.0 + 0.18 * jax.random.normal(key_list[17], (D,), jnp.float32), 0.1, 1.9),
        "expand_weight": bell_draw(key_list[18], (D, FF), D ** -0.5, 0.25),
        "reduce_weight": bell_draw(key_list[19], (FF, D), FF ** -0.5, 0.125),
        "gain_final": jnp.clip(1.0 + 0.18 * jax.random.normal(key_list[20], (D,), jnp.float32), 0.1, 1.9),
        "velocity_head": bell_draw(key_list[21], (D,), D ** -0.5, 0.25, (), jnp.float32),
    }


EPS = 1e-06

def normalize(hidden, gain):
    return hidden * lax.rsqrt(lax.optimization_barrier(jnp.mean(hidden * hidden, -1, keepdims=True)) + EPS) * gain

def head_norm(values):
    split = values.reshape(values.shape[:-1] + (HEADS, HDIM))
    return split * lax.rsqrt(lax.optimization_barrier(jnp.mean(split * split, -1, keepdims=True)) + EPS)

def condition(energy_bin, time_index, energy_table):
    onehot = (jnp.arange(NBINS)[None, :] == energy_bin[:, None])[:, :, None]
    picked = lax.optimization_barrier(jnp.sum(jnp.where(onehot, energy_table[None], 0.0), 1))
    moment = time_index[0].astype(jnp.float32) / GRID
    freqs = jnp.exp(-math.log(1000.0) * jnp.arange(D // 2).astype(jnp.float32) / (D // 2))
    angles = moment * 100.0 * freqs
    return picked + jnp.concatenate([jnp.sin(angles), jnp.cos(angles)])[None]

def attend(queries, keys, values, scale, allowed):
    scores = jnp.einsum('qhd,khd->hqk', queries.astype(jnp.float32), keys.astype(jnp.float32))
    scores = scores * (scale[:, None, None] / math.sqrt(HDIM))
    scores = jnp.where(allowed[None], scores, -1e+30)
    top = lax.optimization_barrier(jnp.max(scores, -1, keepdims=True))
    weights = jnp.exp(scores - top)
    total = lax.optimization_barrier(jnp.sum(weights, -1))
    rounded = lax.optimization_barrier(weights.astype(jnp.bfloat16)).astype(jnp.float32)
    mixed = jnp.einsum('hqk,khd->qhd', rounded, values.astype(jnp.float32))
    mixed = mixed / jnp.transpose(total)[:, :, None]
    return mixed.reshape(mixed.shape[0], D).astype(jnp.bfloat16)

def project(normed, heads):
    proj = jnp.dot(normed, heads, preferred_element_type=jnp.float32)
    queries = head_norm(proj[:, :D]).astype(jnp.bfloat16)
    keys = head_norm(proj[:, D:2 * D]).astype(jnp.bfloat16)
    values = proj[:, 2 * D:].reshape(proj.shape[0], HEADS, HDIM).astype(jnp.bfloat16)
    return (queries, keys, values)

def reference(shower_state, cell_valid, layer_valid, energy_bin, time_index, embed_weight, cell_embed, layer_embed, energy_table, gain_cells, cell_heads, cell_merge, cell_scale, gain_layers, layer_heads, layer_merge, layer_scale, gain_expand, expand_weight, reduce_weight, gain_final, velocity_head):
    cell_ok = cell_valid == 1
    layer_ok = layer_valid == 1
    cond = condition(energy_bin, time_index, energy_table)
    hidden = shower_state[..., None] * embed_weight + cell_embed[None, None] + layer_embed[None, :, None] + cond[:, None, None]
    normed = normalize(hidden, gain_cells).astype(jnp.bfloat16)
    cell_allowed = cell_ok[None, :] | jnp.eye(CELLS, dtype=bool)

    def in_layer(rows):
        queries, keys, values = project(rows, cell_heads)
        return attend(queries, keys, values, cell_scale, cell_allowed)
    mixed = lax.map(in_layer, normed.reshape(SHOWERS * LAYERS, CELLS, D)).reshape(SHOWERS, LAYERS, CELLS, D)
    hidden = hidden + jnp.dot(mixed, cell_merge, preferred_element_type=jnp.float32)
    normed = normalize(hidden, gain_layers).astype(jnp.bfloat16)
    layer_allowed = layer_ok[None, :] | jnp.eye(LAYERS, dtype=bool)

    def across(rows):
        queries, keys, values = project(rows, layer_heads)
        return attend(queries, keys, values, layer_scale, layer_allowed)
    columns = jnp.swapaxes(normed, 1, 2).reshape(SHOWERS * CELLS, LAYERS, D)
    mixed = jnp.swapaxes(lax.map(across, columns).reshape(SHOWERS, CELLS, LAYERS, D), 1, 2)
    hidden = hidden + jnp.dot(mixed, layer_merge, preferred_element_type=jnp.float32)
    normed = normalize(hidden, gain_expand).astype(jnp.bfloat16)
    inner = jax.nn.gelu(jnp.dot(normed, expand_weight, preferred_element_type=jnp.float32)).astype(jnp.bfloat16)
    hidden = hidden + jnp.dot(inner, reduce_weight, preferred_element_type=jnp.float32)
    velocity = lax.optimization_barrier(jnp.sum(normalize(hidden, gain_final) * velocity_head, -1))
    velocity = velocity * cell_ok[None, None, :].astype(jnp.float32) * layer_ok[None, :, None].astype(jnp.float32)
    return (velocity, shower_state + velocity / STEPS)
```

```python
import functools
import math

import jax
import jax.numpy as jnp
from jax import lax
from jax.experimental import pallas as pl
from jax.experimental.pallas import tpu as pltpu
from jax.sharding import PartitionSpec as P

D = 512
HEADS = 8
HDIM = 64
NBINS = 64
GRID = 1000
STEPS = 2
EPS = 1e-06
LOG2E = math.log2(math.e)
F32 = jnp.float32
BF16 = jnp.bfloat16
MESH = pl.DeviceIdType.MESH
NT = (((1,), (1,)), ((), ()))


def iota(shape, axis):
    return lax.broadcasted_iota(jnp.int32, shape, axis)


def normed(hidden, gain):
    scale = lax.rsqrt(jnp.mean(hidden * hidden, -1, keepdims=True) + EPS)
    return (hidden * scale * gain).astype(BF16)


def head_norm_t(proj):
    parts = []
    for h in range(proj.shape[0] // HDIM):
        rows = proj[h * HDIM : (h + 1) * HDIM]
        scale = lax.rsqrt(jnp.mean(rows * rows, 0, keepdims=True) + EPS)
        parts.append(rows * scale)
    return parts


def kernel(
    bins,
    time,
    cell_scale,
    layer_scale,
    state,
    cell_valid,
    layer_valid,
    embed_w,
    cell_e,
    layer_e,
    table,
    gain1,
    gain2,
    gain3,
    gain4,
    vhead,
    heads1_h,
    merge1_h,
    heads2_h,
    merge2_h,
    expand_h,
    reduce_h,
    vel_out,
    next_out,
    heads1,
    merge1,
    heads2,
    merge2,
    expand,
    reduce,
    qkt1,
    qkt2,
    square,
    sx,
    ceb,
    leb,
    sdb,
    a1,
    kt,
    va,
    mask1,
    oacc,
    obuf,
    rbuf,
    o1,
    hid,
    vsend,
    vrecv,
    wsem,
    zs,
    zr,
    xs,
    xr,
    cs,
    cr,
    ls,
    lr,
    ss,
    sr,
    as_,
    ar,
    fs,
    fr,
):
    lam = lax.axis_index("layer")
    ci = lax.axis_index("cell")
    core = lax.rem(ci, 2)
    col = ci // 2
    x = lax.rem(col, 4)
    z = col // 4
    qb = col // 2
    b = lax.rem(col, 2)
    rank = lam * 2 + core

    z_dev = [(lam, (lax.rem(z + d, 4) * 4 + x) * 2 + core) for d in (1, 2, 3)]
    x_dev = [(lam, (z * 4 + lax.rem(x + d, 4)) * 2 + core) for d in (1, 3, 2)]
    sibling = (lam, col * 2 + 1 - core)
    quarter = lax.rem(ci, 4)
    holder = []
    for sb in range(2):
        for k in range(4):
            r = quarter * 4 + k
            holder.append((r // 2, (qb * 2 + sb) * 2 + lax.rem(r, 2)))
    owner = [(l, qb * 4 + rank // 4) for l in range(8)]

    def is_me(dev):
        return jnp.logical_and(dev[0] == lam, dev[1] == ci)

    barrier = pltpu.get_barrier_semaphore()

    def greet(dev):
        pl.semaphore_signal(barrier, inc=1, device_id=dev, device_id_type=MESH)

    for dev in z_dev + x_dev:
        greet(dev)
    for i in range(1, 16):
        r = lax.rem(rank + i, 16)
        greet((r // 2, col * 2 + lax.rem(r, 2)))
    for dev in holder + owner:

        @pl.when(jnp.logical_not(is_me(dev)))
        def _():
            greet(dev)

    selves = sum(jnp.where(is_me(dev), 1, 0) for dev in holder + owner)

    weights = [
        pltpu.make_async_copy(src, dst, wsem.at[i])
        for i, (src, dst) in enumerate(
            (
                (heads1_h, heads1),
                (merge1_h, merge1),
                (heads2_h, heads2),
                (merge2_h, merge2),
                (expand_h, expand),
                (reduce_h, reduce),
            )
        )
    ]
    for copy in weights:
        copy.start()

    square[...] = jnp.zeros_like(square)
    square[0:6, 0:32] = state[0]
    square[8:14, 0:32] = state[1]
    turned = jnp.transpose(square[...])[0:32]
    hit = iota((32, 1024), 1) == ci * 32 + iota((32, 1024), 0)
    own_ok = jnp.sum(jnp.where(hit, cell_valid[...].astype(F32), 0.0), -1, keepdims=True)
    lane = iota((32, 128), 1)
    sx[0] = turned
    sx[1] = pltpu.roll(turned, 120, 1)
    ceb[x, core, z, :, 0:D] = cell_e[...]
    ceb[x, core, z, :, D : D + 128] = jnp.where(lane == 16, own_ok, turned)
    leb[lam, 0:6, :] = layer_e[...]

    pl.semaphore_wait(barrier, 37 - selves)

    def push(src, dst, send, recv, dev):
        return pltpu.make_async_remote_copy(
            src_ref=src, dst_ref=dst, send_sem=send, recv_sem=recv, device_id=dev, device_id_type=MESH
        )

    z_out = []
    for i, dev in enumerate(z_dev):
        slot = ceb.at[x, core, z]
        z_out.append(push(slot, slot, zs.at[i], zr.at[i], dev))
        z_out[-1].start()

    for i, dev in enumerate(holder):
        src = sx.at[i // 4, pl.ds((i % 4) * 8, 8)]

        @pl.when(jnp.logical_not(is_me(dev)))
        def _():
            push(src, sdb.at[lam], ss.at[i], sr.at[lam], dev).start()

        @pl.when(is_me(dev))
        def _():
            sdb[lam] = sx[i // 4, (i % 4) * 8 : (i % 4) * 8 + 8]

    for i in range(1, 8):
        l = lax.rem(lam + i, 8)
        push(leb.at[lam], leb.at[lam], ls.at[i], lr.at[i], (l, ci)).start()

    picked = table[pl.ds(bins[b], 1), :]
    position = iota((1, D), 1)
    power = jnp.where(position < D // 2, position, position - D // 2).astype(F32)
    freqs = jnp.exp(-math.log(1000.0) * power / (D // 2))
    moment = jnp.full((1, D), time[0], jnp.int32).astype(F32) / GRID
    angles = moment * 100.0 * freqs
    cond = picked + jnp.where(position < D // 2, jnp.sin(angles), jnp.cos(angles))

    weights[0].wait()
    qkt1[...] = jnp.transpose(heads1[:, 0 : 2 * D])

    def block(l, chunk):
        rows = ceb[chunk].reshape(256, D + 128)
        lanes = pltpu.roll(rows[:, D:], lax.rem(128 - (b * 8 + core * 3 + l), 128), 1)
        hidden = lanes[:, 0:1] * embed_w[...] + rows[:, 0:D] + layer_e[pl.ds(core * 3 + l, 1), :] + cond
        act = normed(hidden, gain1[...])
        a1[l, chunk] = act.reshape(2, 4, 32, D)
        keys = lax.dot_general(qkt1[D : 2 * D], act, NT, preferred_element_type=F32)
        for h, part in enumerate(head_norm_t(keys)):
            kt[l, chunk, h * HDIM : (h + 1) * HDIM, :] = part.astype(BF16)
        va[l, chunk] = jnp.dot(act, heads1[:, 2 * D : 3 * D], preferred_element_type=F32).astype(BF16)

    def blocks(chunk):
        lax.fori_loop(0, 3, lambda l, _: (block(l, chunk), 0)[1], 0)

    for i, copy in enumerate(z_out):
        zz = lax.rem(z + 4 - (i + 1), 4)
        slot = ceb.at[x, core, zz]
        push(slot, slot, zs.at[i], zr.at[i], z_dev[i]).wait_recv()
    x_out = []
    for i, dev in enumerate(x_dev):
        slot = ceb.at[x, core]
        x_out.append(push(slot, slot, xs.at[i], xr.at[i], dev))
        x_out[-1].start()

    def to_sibling(n, chunk):
        mine = ceb.at[chunk, core]
        push(mine, mine, cs.at[n], cr.at[n], sibling).start()

    def from_sibling(n, chunk):
        theirs = ceb.at[chunk, 1 - core]
        push(theirs, theirs, cs.at[n], cr.at[n], sibling).wait_recv()

    to_sibling(0, x)
    from_sibling(0, x)
    blocks(x)
    chunks = [x] + [lax.rem(x + 4 - d, 4) for d in (1, 3, 2)]
    for n in (1, 2, 3):
        slot = ceb.at[chunks[n], core]
        push(slot, slot, xs.at[n - 1], xr.at[n - 1], x_dev[n - 1]).wait_recv()
        to_sibling(n, chunks[n])
        from_sibling(n, chunks[n])
        blocks(chunks[n])

    for c in range(4):
        side = jnp.transpose(ceb[c].reshape(256, D + 128)[:, D:])
        key_ok = side[16:17] > 0.5
        pos = iota((128, 256), 1)
        key = (lax.rem(pos // 32, 4) * 4 + c) * 64 + (pos // 128) * 32 + lax.rem(pos, 32)
        query = qb * 128 + iota((128, 256), 0)
        mask1[c] = jnp.where(jnp.logical_or(key_ok, key == query), 0.0, -1e30)

    pair = (x // 2) * 2

    def attend1(l, _):
        act = jnp.concatenate([a1[l, pair + i // 2, i % 2, z] for i in range(4)], 0)
        proj = lax.dot_general(qkt1[0:D], act, NT, preferred_element_type=F32)
        queries = head_norm_t(proj)
        for h in range(HEADS):
            query = jnp.transpose(queries[h]).astype(BF16)
            factor = cell_scale[h] * (LOG2E / math.sqrt(HDIM))
            scores = [
                jnp.dot(query, kt[l, c, h * HDIM : (h + 1) * HDIM, :], preferred_element_type=F32) + mask1[c]
                for c in range(4)
            ]
            top = jnp.maximum(jnp.maximum(scores[0], scores[1]), jnp.maximum(scores[2], scores[3]))
            top = jnp.max(top, -1, keepdims=True)
            total = jnp.zeros((128, 256), F32)
            mixed = jnp.zeros((128, 128), F32)
            first = (h // 2) * 128
            for c in range(4):
                p = jnp.exp2((scores[c] - top) * factor)
                total = total + p
                mixed = mixed + jnp.dot(
                    p.astype(BF16), va[l, c, :, first : first + 128], preferred_element_type=F32
                )
            mixed = mixed / jnp.sum(total, -1, keepdims=True)
            if h % 2 == 0:
                even = mixed
            else:
                oacc[l, :, first : first + 128] = jnp.where(iota((128, 128), 1) < HDIM, even, mixed)
        return 0

    lax.fori_loop(0, 3, attend1, 0)

    def fill(r, _):
        rows = pl.ds(pl.multiple_of(r * 8, 8), 8)
        obuf[r, :, 0:D] = jnp.concatenate([oacc[0, rows, :], oacc[1, rows, :]], 0).astype(BF16)
        last = oacc[2, rows, :]
        obuf[r, :, D : D + 256] = jnp.concatenate([last[:, 0:256], last[:, 256:D]], 0).astype(BF16)
        return 0

    lax.fori_loop(0, 16, fill, 0)
    for i in range(1, 16):
        r = lax.rem(rank + i, 16)
        push(obuf.at[r], rbuf.at[rank], as_.at[i], ar.at[i], (r // 2, col * 2 + lax.rem(r, 2))).start()
    rbuf[rank] = obuf[rank]

    weights[2].wait()
    qkt2[...] = jnp.transpose(heads2[:, 0 : 2 * D])
    for i in range(8):
        dev = owner[i]

        @pl.when(jnp.logical_not(is_me(dev)))
        def _():
            push(sx.at[0, pl.ds(0, 8)], sdb.at[i], ss.at[i], sr.at[i], dev).wait_recv()

    for i in range(1, 8):
        l = lax.rem(lam + 8 - i, 8)
        push(leb.at[l], leb.at[l], ls.at[i], lr.at[i], (l, ci)).wait_recv()

    eighth = lax.rem(rank, 4)
    ce8 = ceb[pair + rank // 8, lax.rem(rank // 4, 2), z, pl.ds(pl.multiple_of(eighth * 8, 8), 8), 0:D] + cond
    for l in range(48):
        column = sdb[l // 6][:, l % 6 : l % 6 + 1]
        hid[l * 8 : l * 8 + 8, :] = column * embed_w[...] + ce8 + leb[l // 6, l % 6 : l % 6 + 1, :]

    spread = (iota((48, 384), 1) // 8 == iota((48, 384), 0)).astype(BF16)
    layer_ok = jnp.dot(layer_valid[...].astype(F32).astype(BF16), spread, preferred_element_type=F32) > 0.5
    rows, cols = iota((384, 384), 0), iota((384, 384), 1)
    same = lax.rem(rows, 8) == lax.rem(cols, 8)
    allowed = jnp.logical_and(same, jnp.logical_or(layer_ok, rows == cols))
    mask2 = jnp.where(allowed, 0.0, -1e30)

    for i in range(1, 16):
        r = lax.rem(rank + 16 - i, 16)
        push(obuf.at[r], rbuf.at[r], as_.at[i], ar.at[i], (r // 2, col * 2 + lax.rem(r, 2))).wait_recv()

    for s in range(8):
        parts = []
        for i in (2 * s, 2 * s + 1):
            got = rbuf[i].astype(F32)
            parts += [got[:, 0:D], jnp.concatenate([got[0:8, D:], got[8:16, D:]], 1)]
        o1[48 * s : 48 * s + 48, :] = jnp.concatenate(parts, 0).astype(BF16)

    weights[1].wait()
    hidden = hid[...] + jnp.dot(o1[...], merge1[...], preferred_element_type=F32)
    hid[...] = hidden
    act = normed(hidden, gain2[...])
    proj = head_norm_t(lax.dot_general(qkt2[...], act, NT, preferred_element_type=F32))
    values = jnp.dot(act, heads2[:, 2 * D : 3 * D], preferred_element_type=F32).astype(BF16)
    for h in range(HEADS):
        query = jnp.transpose(proj[h]).astype(BF16)
        factor = layer_scale[h] * (LOG2E / math.sqrt(HDIM))
        scores = jnp.dot(query, proj[HEADS + h].astype(BF16), preferred_element_type=F32) + mask2
        top = jnp.max(scores, -1, keepdims=True)
        p = jnp.exp2((scores - top) * factor)
        first = (h // 2) * 128
        mixed = jnp.dot(p.astype(BF16), values[:, first : first + 128], preferred_element_type=F32)
        mixed = mixed / jnp.sum(p, -1, keepdims=True)
        if h % 2 == 0:
            even = mixed
        else:
            o1[:, first : first + 128] = jnp.where(iota((384, 128), 1) < HDIM, even, mixed).astype(BF16)

    weights[3].wait()
    hidden = hid[...] + jnp.dot(o1[...], merge2[...], preferred_element_type=F32)
    act = normed(hidden, gain3[...])
    weights[4].wait()
    weights[5].wait()
    for c in range(4):
        inner = jnp.dot(act, expand[:, c * 512 : c * 512 + 512], preferred_element_type=F32)
        inner = jax.nn.gelu(inner).astype(BF16)
        hidden = hidden + jnp.dot(inner, reduce[c * 512 : c * 512 + 512, :], preferred_element_type=F32)

    scale = lax.rsqrt(jnp.mean(hidden * hidden, -1, keepdims=True) + EPS)
    velocity = scale * jnp.sum(hidden * (gain4[...] * vhead[...]), -1, keepdims=True)
    lane = iota((8, 128), 1)
    tile = jnp.zeros((8, 128), F32)
    for l in range(48):
        tile = jnp.where(lane == l, velocity[l * 8 : l * 8 + 8], tile)
    first = qb * 128 + rank * 8
    hit = iota((8, 1024), 1) == first + iota((8, 1024), 0)
    cell_ok = jnp.sum(jnp.where(hit, cell_valid[...].astype(F32), 0.0), -1, keepdims=True)
    tile = tile * cell_ok
    for l in range(8):
        vsend[l] = tile if l == 0 else pltpu.roll(tile, 128 - 6 * l, 1)

    slot = b * 4 + eighth
    for l in range(8):
        dev = owner[l]

        @pl.when(jnp.logical_not(is_me(dev)))
        def _():
            push(vsend.at[l], vrecv.at[slot], fs.at[l], fr.at[slot], dev).start()

        @pl.when(is_me(dev))
        def _():
            vrecv[slot] = vsend[l]

    for i, dev in enumerate(holder):

        @pl.when(jnp.logical_not(is_me(dev)))
        def _():
            push(vsend.at[0], vrecv.at[i], fs.at[0], fr.at[i], dev).wait_recv()

    own = layer_valid[...]
    hit = iota((8, 48), 1) == lam * 6 + iota((8, 48), 0)
    own_layer = jnp.sum(jnp.where(hit, own.astype(F32), 0.0), -1, keepdims=True)[0:6]
    for sb in range(2):
        square[0:32, :] = vrecv[4 * sb : 4 * sb + 4].reshape(32, 128)
        vel = jnp.transpose(square[...])[0:6, 0:32] * own_layer
        vel_out[sb] = vel
        next_out[sb] = state[sb] + vel / STEPS

    for copy in z_out + x_out:
        copy.wait_send()
    for n in range(4):
        mine = ceb.at[chunks[n], core]
        push(mine, mine, cs.at[n], cr.at[n], sibling).wait_send()
    for i, dev in enumerate(holder):

        @pl.when(jnp.logical_not(is_me(dev)))
        def _():
            push(sx.at[0, pl.ds(0, 8)], sdb.at[lam], ss.at[i], sr.at[lam], dev).wait_send()

    for i in range(1, 8):
        push(leb.at[lam], leb.at[lam], ls.at[i], lr.at[i], (lax.rem(lam + i, 8), ci)).wait_send()
    for i in range(1, 16):
        r = lax.rem(rank + i, 16)
        push(obuf.at[r], rbuf.at[rank], as_.at[i], ar.at[i], (r // 2, col * 2 + lax.rem(r, 2))).wait_send()
    for l in range(8):
        dev = owner[l]

        @pl.when(jnp.logical_not(is_me(dev)))
        def _():
            push(vsend.at[l], vrecv.at[slot], fs.at[l], fr.at[slot], dev).wait_send()


def on_device(
    shower_state,
    cell_valid,
    layer_valid,
    energy_bin,
    time_index,
    embed_weight,
    cell_embed,
    layer_embed,
    energy_table,
    gain_cells,
    cell_heads,
    cell_merge,
    cell_scale,
    gain_layers,
    layer_heads,
    layer_merge,
    layer_scale,
    gain_expand,
    expand_weight,
    reduce_weight,
    gain_final,
    velocity_head,
):
    row = lambda v: v.reshape(1, -1)
    smem = pl.BlockSpec(memory_space=pltpu.SMEM)
    vmem = pl.BlockSpec(memory_space=pltpu.VMEM)
    hbm = pl.BlockSpec(memory_space=pl.ANY)
    dma = lambda n: pltpu.SemaphoreType.DMA((n,))
    shape = jax.ShapeDtypeStruct(shower_state.shape, F32)
    return pl.pallas_call(
        kernel,
        out_shape=(shape, shape),
        in_specs=[smem] * 4 + [vmem] * 12 + [hbm] * 6,
        out_specs=(vmem, vmem),
        scratch_shapes=[
            pltpu.VMEM((D, 3 * D), BF16),
            pltpu.VMEM((D, D), BF16),
            pltpu.VMEM((D, 3 * D), BF16),
            pltpu.VMEM((D, D), BF16),
            pltpu.VMEM((D, 4 * D), BF16),
            pltpu.VMEM((4 * D, D), BF16),
            pltpu.VMEM((2 * D, D), BF16),
            pltpu.VMEM((2 * D, D), BF16),
            pltpu.VMEM((128, 128), F32),
            pltpu.VMEM((2, 32, 128), F32),
            pltpu.VMEM((4, 2, 4, 32, D + 128), F32),
            pltpu.VMEM((8, 8, D), F32),
            pltpu.VMEM((8, 8, 128), F32),
            pltpu.VMEM((3, 4, 2, 4, 32, D), BF16),
            pltpu.VMEM((3, 4, D, 256), BF16),
            pltpu.VMEM((3, 4, 256, D), BF16),
            pltpu.VMEM((4, 128, 256), F32),
            pltpu.VMEM((3, 128, D), F32),
            pltpu.VMEM((16, 16, D + 256), BF16),
            pltpu.VMEM((16, 16, D + 256), BF16),
            pltpu.VMEM((384, D), BF16),
            pltpu.VMEM((384, D), F32),
            pltpu.VMEM((8, 8, 128), F32),
            pltpu.VMEM((8, 8, 128), F32),
        ]
        + [dma(n) for n in (6, 3, 3, 3, 3, 4, 4, 8, 8, 8, 8, 16, 16, 8, 8)],
        compiler_params=pltpu.CompilerParams(
            collective_id=0, has_side_effects=True, vmem_limit_bytes=56 * 1024 * 1024
        ),
    )(
        energy_bin,
        time_index,
        cell_scale,
        layer_scale,
        shower_state,
        row(cell_valid),
        row(layer_valid),
        row(embed_weight),
        cell_embed,
        layer_embed,
        energy_table,
        row(gain_cells),
        row(gain_layers),
        row(gain_expand),
        row(gain_final),
        row(velocity_head),
        cell_heads,
        cell_merge,
        layer_heads,
        layer_merge,
        expand_weight,
        reduce_weight,
    )


def solution(mesh):
    return jax.shard_map(
        on_device,
        mesh=mesh,
        in_specs=(
            P(None, "layer", "cell"),
            P(),
            P(),
            P(),
            P(),
            P(),
            P("cell", None),
            P("layer", None),
        )
        + (P(),) * 14,
        out_specs=(P(None, "layer", "cell"), P(None, "layer", "cell")),
        check_vma=False,
    )
```
